256 devices in a mesh: height: 32 (over z_hi, x, core), plan: 8 (over z_lo, y).
Axes of the slice: x: 4, y: 4, z: 8 (z_hi: 4, z_lo: 2; z = z_hi * 2 + z_lo), core: 2. Of those that a mesh axis runs over, the one named last changes fastest.
Arguments:
- displacement: float32 [3, 32, 40, 1024], P(None, 'height', None, 'plan'), may hold values from -3 to 3
- velocity: float32 [3, 32, 40, 1024], P(None, 'height', None, 'plan'), may hold values from -3 to 3
- lumped_mass: float32 [32, 40, 1024], P('height', None, 'plan'), may hold values from 0.3 to 3
- plastic_strain: float32 [3, 8, 32, 40, 1024], P(None, None, 'height', None, 'plan'), may hold values from -1 to 1
- hardening_strain: float32 [3, 8, 32, 40, 1024], P(None, None, 'height', None, 'plan'), may hold values from 0.01 to 0.5
- material_ids: int32 [3, 8, 32, 40, 1024], P(None, None, 'height', None, 'plan'), may hold values from 0 to 7
- material_table: float32 [8, 3], replicated, may hold values from 0.5 to 2
- ground_accel: float32 [4, 3], replicated, may hold values from -4 to 4
- snapshot_history: bfloat16 [60, 3, 32, 40, 1024], P(None, None, 'height', None, 'plan'), may hold values from -6 to 6
- mode_shapes: bfloat16 [256, 3, 32, 40, 1024], P(None, None, 'height', None, 'plan'), as said below
Outputs:
- displacement_end: float32 [3, 32, 40, 1024], P(None, 'height', None, 'plan')
- velocity_end: float32 [3, 32, 40, 1024], P(None, 'height', None, 'plan')
- plastic_end: float32 [3, 8, 32, 40, 1024], P(None, None, 'height', None, 'plan')
- hardening_end: float32 [3, 8, 32, 40, 1024], P(None, None, 'height', None, 'plan')
- modal_coords: float32 [256, 64], P(('height', 'plan'))
The draws below stay inside these ranges and needn't reach their ends.
Inputs may be any that keep to these rules, and one draw needn't show every extreme that they name: mode_shapes are scaled so that mass_gram is positive definite and well conditioned.
All inputs are finite; a program needn't handle non-finite values.
Results may differ from the reference program's by a relative error of at most 0.0083.
Values sent between devices are 32-bit elements; how exact they have to be, the bound alone decides.
No kernel may reach another device: no remote copies, remote signals or barrier semaphores. Data moves between devices by JAX's collectives and lax.ppermute only.
A program may use at most 128 MiB of HBM per device.

```python
import math
import jax
import jax.numpy as jnp
from jax import lax

MODES = 256
SNAP = 64
STEPS = 4
NF = 8
NMAT = 8
QY = 40
HIST = 60
NZ = 32
NP = 1024


def draw_mode_shapes(key, part):
    array_shape = (MODES, 3, NZ, QY, NP)
    unit_scale = (3 * NZ * QY * NP) ** (-0.5)
    raw_values = jax.random.normal(key, array_shape, jnp.float32)
    partner = jax.random.permutation(jax.random.fold_in(key, 13), MODES)
    mixed_modes = raw_values + 0.6 * jnp.take(raw_values, partner, axis=0)
    return (mixed_modes * unit_scale).astype(jnp.bfloat16)


def set_ends(array, own_key, low, top_value):
    longest = array.shape.index(max(array.shape))
    spots = []
    for shift in (0, 1):
        where = [jax.random.randint(jax.random.fold_in(own_key, axis), (), 0, length) for axis, length in enumerate(array.shape)]
        where[longest] = (where[longest] + shift) % array.shape[longest]
        spots.append(tuple(where))
    return array.at[spots[0]].set(low).at[spots[1]].set(top_value)


def level_of(rng, extent, shards, least, top_value):
    level = 1.0
    for axis_at, blocks in shards:
        steps = jax.random.uniform(jax.random.fold_in(jax.random.fold_in(rng, 6), axis_at), (blocks,), jnp.float32, least / len(shards), top_value / len(shards))
        level = level * jnp.repeat(jnp.exp(steps), extent[axis_at] // blocks).reshape((-1,) + (1,) * (len(extent) - 1 - axis_at))
    return level


def gaussian(stream_key, dims, spread, most, cuts=(), held_as=jnp.bfloat16):
    entries = jax.random.normal(stream_key, dims, jnp.float32) * spread
    if len(cuts) > 0:
        entries = level_of(stream_key, dims, cuts, -0.22, 0.18) * entries
    return jnp.clip(entries, min=-most, max=most).astype(held_as)


def setup_inputs(seed: int = 0) -> dict:
    arg_keys = jax.random.split(jax.random.key(seed), 11)
    return {
        "displacement": gaussian(arg_keys[0], (3, NZ, QY, NP), 0.5, 3.0, ((1, 32), (3, 8)), jnp.float32),
        "velocity": gaussian(arg_keys[1], (3, NZ, QY, NP), 0.5, 3.0, ((1, 32), (3, 8)), jnp.float32),
        "lumped_mass": jnp.clip(jnp.exp(math.log(3.0) - 2.3025851 * jax.random.uniform(arg_keys[2], (NZ, QY, NP), jnp.float32) ** level_of(arg_keys[2], (NZ, QY, NP), ((0, 32), (2, 8)), -0.2, 0.2)), 0.3, 3.0),
        "plastic_strain": gaussian(arg_keys[3], (3, NF, NZ, QY, NP), 0.2, 1.0, ((2, 32), (4, 8)), jnp.float32),
        "hardening_strain": jnp.clip(jnp.exp(math.log(0.5) - 3.912023 * jax.random.uniform(arg_keys[4], (3, NF, NZ, QY, NP), jnp.float32) ** level_of(arg_keys[4], (3, NF, NZ, QY, NP), ((2, 32), (4, 8)), -0.2, 0.2)), 0.01, 0.5),
        "material_ids": set_ends(jax.random.randint(arg_keys[5], (3, NF, NZ, QY, NP), 0, NMAT), jax.random.fold_in(arg_keys[5], 1), 0, NMAT - 1).astype(jnp.int32),
        "material_table": jnp.clip(jnp.exp(jax.random.uniform(arg_keys[6], (NMAT, 3), jnp.float32, math.log(0.5), math.log(2.0))), 0.5, 2.0),
        "ground_accel": gaussian(arg_keys[7], (STEPS, 3), 1.0, 4.0, (), jnp.float32),
        "snapshot_history": gaussian(arg_keys[8], (HIST, 3, NZ, QY, NP), 1.0, 6.0, ((2, 32), (4, 8))),
        "mode_shapes": draw_mode_shapes(jax.random.fold_in(arg_keys[10], 71), 0),
    }


time_step = 0.3
mass_damping = 0.1
stiff_damping = 0.05
shear_stiff = 0.5
axial_components = (2, 1, 0)

def fibre_props(material_ids, material_table):
    modulus = jnp.zeros(material_ids.shape, jnp.float32)
    yields = jnp.zeros(material_ids.shape, jnp.float32)
    slopes = jnp.zeros(material_ids.shape, jnp.float32)
    for material_index in range(material_table.shape[0]):
        selected = (material_ids == material_index).astype(jnp.float32)
        modulus = modulus + selected * material_table[material_index, 0]
        yields = yields + selected * (0.4 * material_table[material_index, 1])
        slopes = slopes + selected * (0.1 * material_table[material_index, 2])
    return (modulus, yields, slopes)

def bar_update(stretch, stretch_rate, plastic, harden, modulus, yields, slopes, axial_index):
    trial_stress = modulus * (stretch[axial_index][None] - plastic)
    excess = jnp.abs(trial_stress) - (yields + slopes * harden)
    growth = jnp.maximum(excess, 0.0) / (modulus + slopes)
    flow_sign = jnp.sign(trial_stress)
    plastic_new = plastic + growth * flow_sign
    harden_new = harden + growth
    stress = trial_stress - modulus * growth * flow_sign
    axial_force = jnp.mean(stress, axis=0)
    tangent = jnp.mean(modulus, axis=0)
    component_list = []
    for component in range(3):
        if component == axial_index:
            component_list.append(axial_force + stiff_damping * tangent * stretch_rate[component])
        else:
            component_list.append(shear_stiff * (stretch[component] + stiff_damping * stretch_rate[component]))
    return (jnp.stack(component_list), plastic_new, harden_new)

def earlier_of(bar_index, field):
    if bar_index == 0:
        return jnp.concatenate([jnp.zeros_like(field[:, :1]), field[:, :-1]], axis=1)
    if bar_index == 1:
        return jnp.concatenate([jnp.zeros_like(field[:, :, :1]), field[:, :, :-1]], axis=2)
    return jnp.roll(field, 1, axis=3)

def later_of(bar_index, field):
    if bar_index == 0:
        return jnp.concatenate([field[:, 1:], jnp.zeros_like(field[:, :1])], axis=1)
    if bar_index == 1:
        return jnp.concatenate([field[:, :, 1:], jnp.zeros_like(field[:, :, :1])], axis=2)
    return jnp.roll(field, -1, axis=3)

def reference(displacement, velocity, lumped_mass, plastic_strain, hardening_strain, material_ids, material_table, ground_accel, snapshot_history, mode_shapes):
    modulus, yields, slopes = fibre_props(material_ids, material_table)
    disp_now, velo_now = (displacement, velocity)
    plastic_now, harden_now = (plastic_strain, hardening_strain)
    new_snapshots = []
    for step_index in range(STEPS):
        bar_forces, plastic_parts, harden_parts = ([], [], [])
        for bar_index in range(3):
            bar_force, plastic_part, harden_part = bar_update(disp_now - earlier_of(bar_index, disp_now), velo_now - earlier_of(bar_index, velo_now), plastic_now[bar_index], harden_now[bar_index], modulus[bar_index], yields[bar_index], slopes[bar_index], axial_components[bar_index])
            bar_forces.append(bar_force)
            plastic_parts.append(plastic_part)
            harden_parts.append(harden_part)
        plastic_now = jnp.stack(plastic_parts)
        harden_now = jnp.stack(harden_parts)
        resisting = jnp.zeros_like(disp_now)
        for bar_index in range(3):
            resisting = resisting + bar_forces[bar_index] - later_of(bar_index, bar_forces[bar_index])
        acceleration = -ground_accel[step_index][:, None, None, None] - resisting / lumped_mass[None]
        velo_now = ((1.0 - 0.5 * mass_damping * time_step) * velo_now + time_step * acceleration) / (1.0 + 0.5 * mass_damping * time_step)
        disp_now = disp_now + time_step * velo_now
        new_snapshots.append(disp_now.astype(jnp.bfloat16))
    snapshots = jnp.concatenate([snapshot_history, jnp.stack(new_snapshots)], axis=0)

    def accumulate(level_index, carry):
        mass_gram, projected = carry
        modes_level = lax.dynamic_slice_in_dim(mode_shapes, level_index, 1, axis=2)
        mass_level = lax.dynamic_slice_in_dim(lumped_mass, level_index, 1, axis=0)
        snaps_level = lax.dynamic_slice_in_dim(snapshots, level_index, 1, axis=2)
        weighted = (modes_level.astype(jnp.float32) * mass_level[None, None]).astype(jnp.bfloat16).reshape(MODES, -1)
        flat_modes = modes_level.reshape(MODES, -1)
        flat_snaps = snaps_level.reshape(SNAP, -1)
        mass_gram = mass_gram + jnp.dot(weighted.astype(jnp.float32), flat_modes.T.astype(jnp.float32), preferred_element_type=jnp.float32)
        projected = projected + jnp.dot(weighted.astype(jnp.float32), flat_snaps.T.astype(jnp.float32), preferred_element_type=jnp.float32)
        return (mass_gram, projected)
    start_carry = (jnp.zeros((MODES, MODES), jnp.float32), jnp.zeros((MODES, SNAP), jnp.float32))
    mass_gram, projected = lax.fori_loop(0, NZ, accumulate, start_carry)
    factor = jnp.linalg.cholesky(mass_gram)
    modal_coords = jax.scipy.linalg.cho_solve((factor, True), projected)
    return (disp_now, velo_now, plastic_now, harden_now, modal_coords)
```

```python
import jax
import jax.numpy as jnp
from jax import lax
from jax.sharding import PartitionSpec as P

time_step = 0.3
mass_damping = 0.1
stiff_damping = 0.05
shear_stiff = 0.5
axial_components = (2, 1, 0)

HEIGHT = ("z_hi", "x", "core")
PLAN = ("z_lo", "y")
FIRST = ("x", "y")
SECOND = ("z_hi", "z_lo", "core")


def passed_along(block, axis, distance):
    devices = range(lax.axis_size(axis))
    route = [(i - distance, i) for i in devices if i - distance in devices]
    return lax.ppermute(block, axis, route)


def from_behind(block, axis, distance):
    devices = range(lax.axis_size(axis))
    route = [((i - distance) % len(devices), i) for i in devices]
    return lax.ppermute(block, axis, route)


def fibre_props(material_ids, material_table):
    modulus = jnp.zeros(material_ids.shape, jnp.float32)
    yields = jnp.zeros(material_ids.shape, jnp.float32)
    slopes = jnp.zeros(material_ids.shape, jnp.float32)
    for material_index in range(material_table.shape[0]):
        selected = (material_ids == material_index).astype(jnp.float32)
        modulus = modulus + selected * material_table[material_index, 0]
        yields = yields + selected * (0.4 * material_table[material_index, 1])
        slopes = slopes + selected * (0.1 * material_table[material_index, 2])
    return (modulus, yields, slopes)


def bar_update(stretch, stretch_rate, plastic, harden, modulus, yields, slopes, axial_index):
    trial_stress = modulus * (stretch[axial_index][None] - plastic)
    excess = jnp.abs(trial_stress) - (yields + slopes * harden)
    growth = jnp.maximum(excess, 0.0) / (modulus + slopes)
    flow_sign = jnp.sign(trial_stress)
    plastic_new = plastic + growth * flow_sign
    harden_new = harden + growth
    stress = trial_stress - modulus * growth * flow_sign
    axial_force = jnp.mean(stress, axis=0)
    tangent = jnp.mean(modulus, axis=0)
    component_list = []
    for component in range(3):
        if component == axial_index:
            component_list.append(axial_force + stiff_damping * tangent * stretch_rate[component])
        else:
            component_list.append(
                shear_stiff * (stretch[component] + stiff_damping * stretch_rate[component])
            )
    return (jnp.stack(component_list), plastic_new, harden_new)


def earlier_fields(field, below_rim, left_rim):
    along_height = jnp.concatenate([below_rim, field[:, :-1]], axis=1)
    along_rows = jnp.concatenate([jnp.zeros_like(field[:, :, :1]), field[:, :, :-1]], axis=2)
    along_rim = jnp.concatenate([left_rim, field[:, :, :, :-1]], axis=3)
    return (along_height, along_rows, along_rim)


def summed_over_devices(mass_gram, projected):
    half = mass_gram.shape[0] // 2
    symmetric = 0.5 * (mass_gram + mass_gram.T)
    packed = jnp.concatenate(
        [
            symmetric[:half, :half],
            symmetric[half:, :half],
            symmetric[half:, half:],
            jnp.concatenate([projected[:half], projected[half:]], axis=1),
        ],
        axis=0,
    )
    first, second = lax.axis_size(FIRST), lax.axis_size(SECOND)
    pieces = packed.reshape(first, packed.shape[0] // first, packed.shape[1])
    own = jnp.sum(lax.all_to_all(pieces, FIRST, 0, 0, tiled=True), axis=0)
    spread = jnp.broadcast_to(own[None], (second,) + own.shape)
    total = jnp.sum(lax.all_to_all(spread, SECOND, 0, 0, tiled=True), axis=0)
    spread = jnp.broadcast_to(total[None], (first,) + total.shape)
    packed = lax.all_to_all(spread, FIRST, 0, 0, tiled=True).reshape(packed.shape)
    low_left = packed[half : 2 * half]
    gram = jnp.concatenate(
        [
            jnp.concatenate([packed[:half], low_left.T], axis=1),
            jnp.concatenate([low_left, packed[2 * half : 3 * half]], axis=1),
        ],
        axis=0,
    )
    tail = packed[3 * half :]
    columns = projected.shape[1]
    return gram, jnp.concatenate([tail[:, :columns], tail[:, columns:]], axis=0)


def body(
    displacement,
    velocity,
    lumped_mass,
    plastic_strain,
    hardening_strain,
    material_ids,
    material_table,
    ground_accel,
    snapshot_history,
    mode_shapes,
):
    modulus, yields, slopes = fibre_props(material_ids, material_table)
    disp_now, velo_now = (displacement, velocity)
    plastic_now, harden_now = (plastic_strain, hardening_strain)
    new_snapshots = []
    for step_index in range(ground_accel.shape[0]):
        below_disp, below_velo = passed_along((disp_now, velo_now), HEIGHT, 1)
        left_disp, left_velo = from_behind(
            (disp_now[:, :, :, -1:], velo_now[:, :, :, -1:]), PLAN, 1
        )
        earlier_disp = earlier_fields(disp_now, below_disp, left_disp)
        earlier_velo = earlier_fields(velo_now, below_velo, left_velo)
        bar_forces, plastic_parts, harden_parts = ([], [], [])
        for bar_index in range(3):
            bar_force, plastic_part, harden_part = bar_update(
                disp_now - earlier_disp[bar_index],
                velo_now - earlier_velo[bar_index],
                plastic_now[bar_index],
                harden_now[bar_index],
                modulus[bar_index],
                yields[bar_index],
                slopes[bar_index],
                axial_components[bar_index],
            )
            bar_forces.append(bar_force)
            plastic_parts.append(plastic_part)
            harden_parts.append(harden_part)
        above_force = passed_along(bar_forces[0], HEIGHT, -1)
        plastic_now = jnp.stack(plastic_parts)
        harden_now = jnp.stack(harden_parts)
        right_force = from_behind(bar_forces[2][:, :, :, :1], PLAN, -1)
        later_height = jnp.concatenate([bar_forces[0][:, 1:], above_force], axis=1)
        later_rows = jnp.concatenate(
            [bar_forces[1][:, :, 1:], jnp.zeros_like(bar_forces[1][:, :, :1])], axis=2
        )
        later_rim = jnp.concatenate([bar_forces[2][:, :, :, 1:], right_force], axis=3)
        resisting = (
            bar_forces[0]
            - later_height
            + (bar_forces[1] - later_rows)
            + (bar_forces[2] - later_rim)
        )
        acceleration = (
            -ground_accel[step_index][:, None, None, None] - resisting / lumped_mass[None]
        )
        velo_now = (
            (1.0 - 0.5 * mass_damping * time_step) * velo_now + time_step * acceleration
        ) / (1.0 + 0.5 * mass_damping * time_step)
        disp_now = disp_now + time_step * velo_now
        new_snapshots.append(disp_now.astype(jnp.bfloat16))
    snapshots = jnp.concatenate([snapshot_history, jnp.stack(new_snapshots)], axis=0)
    mode_count = mode_shapes.shape[0]
    flat_modes = mode_shapes.reshape(mode_count, -1)
    weighted = (
        (mode_shapes.astype(jnp.float32) * lumped_mass[None, None])
        .astype(jnp.bfloat16)
        .reshape(mode_count, -1)
    )
    flat_snaps = snapshots.reshape(snapshots.shape[0], -1)
    contract_last = (((1,), (1,)), ((), ()))
    mass_gram = lax.dot_general(
        weighted, flat_modes, contract_last, preferred_element_type=jnp.float32
    )
    projected = lax.dot_general(
        weighted, flat_snaps, contract_last, preferred_element_type=jnp.float32
    )
    devices_all = lax.axis_size(HEIGHT + PLAN)
    row_count = mode_count // devices_all
    gram_total, projected_total = summed_over_devices(mass_gram, projected)
    factor = jnp.linalg.cholesky(gram_total)
    coords_all = jax.scipy.linalg.cho_solve((factor, True), projected_total)
    modal_coords = lax.dynamic_slice_in_dim(
        coords_all, lax.axis_index(HEIGHT + PLAN) * row_count, row_count, 0
    )
    return (disp_now, velo_now, plastic_now, harden_now, modal_coords)


def solution(mesh):
    split = (4, 4, 2, 2, 4)
    return jax.shard_map(
        body,
        mesh=jax.sharding.Mesh(mesh.devices.reshape(split), HEIGHT + PLAN),
        in_specs=(
            P(None, HEIGHT, None, PLAN),
            P(None, HEIGHT, None, PLAN),
            P(HEIGHT, None, PLAN),
            P(None, None, HEIGHT, None, PLAN),
            P(None, None, HEIGHT, None, PLAN),
            P(None, None, HEIGHT, None, PLAN),
            P(),
            P(),
            P(None, None, HEIGHT, None, PLAN),
            P(None, None, HEIGHT, None, PLAN),
        ),
        out_specs=(
            P(None, HEIGHT, None, PLAN),
            P(None, HEIGHT, None, PLAN),
            P(None, None, HEIGHT, None, PLAN),
            P(None, None, HEIGHT, None, PLAN),
            P(HEIGHT + PLAN, None),
        ),
        check_vma=False,
    )
```

```python
import functools

import jax
import jax.numpy as jnp
from jax import lax
from jax.experimental import pallas as pl
from jax.experimental.pallas import tpu as pltpu
from jax.sharding import PartitionSpec as P

HEIGHT = ("z_hi", "x", "core")
PLAN = ("z_lo", "y")
FIRST = ("x", "y")
SECOND = ("z_hi", "z_lo", "core")

def small_inverse(p):
    r_a = 1.0 / (p[0][0] * p[1][1] - p[1][0] * p[1][0])
    a00, a10, a11 = p[1][1] * r_a, -p[1][0] * r_a, p[0][0] * r_a
    y00 = p[2][0] * a00 + p[2][1] * a10
    y01 = p[2][0] * a10 + p[2][1] * a11
    y10 = p[3][0] * a00 + p[3][1] * a10
    y11 = p[3][0] * a10 + p[3][1] * a11
    s00 = p[2][2] - (y00 * p[2][0] + y01 * p[2][1])
    s10 = p[3][2] - (y10 * p[2][0] + y11 * p[2][1])
    s11 = p[3][3] - (y10 * p[3][0] + y11 * p[3][1])
    r_s = 1.0 / (s00 * s11 - s10 * s10)
    c00, c10, c11 = s11 * r_s, -s10 * r_s, s00 * r_s
    d20 = -(c00 * y00 + c10 * y10)
    d21 = -(c00 * y01 + c10 * y11)
    d30 = -(c10 * y00 + c11 * y10)
    d31 = -(c10 * y01 + c11 * y11)
    d00 = a00 - (y00 * d20 + y10 * d30)
    d10 = a10 - (y01 * d20 + y11 * d30)
    d11 = a11 - (y01 * d21 + y11 * d31)
    return [
        [d00, d10, d20, d30],
        [d10, d11, d21, d31],
        [d20, d21, c00, c10],
        [d30, d31, c10, c11],
    ]


def inverse(rows):
    size = rows[0].shape[1]
    lane = lax.broadcasted_iota(jnp.int32, (1, size), 1)
    lane8 = lax.broadcasted_iota(jnp.int32, (8, size), 1)
    row8 = lax.broadcasted_iota(jnp.int32, (8, size), 0)
    rows = list(rows)
    for step in range(size // 4):
        start = 4 * step
        block, offset = start // 8, start % 8
        pivot = [rows[block][offset + i : offset + i + 1] for i in range(4)]
        entry = [
            [jnp.broadcast_to(pivot[i][:, start + j : start + j + 1], (1, size)) for j in range(i + 1)]
            for i in range(4)
        ]
        inv = small_inverse(entry)
        inside = (lane >= start) & (lane < start + 4)
        unit = [
            jnp.where(inside, (lane == start + j).astype(jnp.float32), pivot[j]) for j in range(4)
        ]
        scaled = [
            (inv[i][0] * unit[0] + inv[i][1] * unit[1]) + (inv[i][2] * unit[2] + inv[i][3] * unit[3])
            for i in range(4)
        ]
        scaled8 = [jnp.broadcast_to(row, (8, size)) for row in scaled]
        inside8 = (lane8 >= start) & (lane8 < start + 4)
        for index in range(len(rows)):
            old = rows[index]
            column = [jnp.broadcast_to(old[:, start + j : start + j + 1], (8, size)) for j in range(4)]
            new = jnp.where(inside8, 0.0, old)
            new = new - (
                (column[0] * scaled8[0] + column[1] * scaled8[1])
                + (column[2] * scaled8[2] + column[3] * scaled8[3])
            )
            if index == block:
                for i in range(4):
                    new = jnp.where(row8 == offset + i, scaled8[i], new)
            rows[index] = new
    return jnp.concatenate(rows, axis=0)


def precise_dot(left, right, contract=(1, 0)):
    return lax.dot_general(
        left,
        right,
        (((contract[0],), (contract[1],)), ((), ())),
        precision=lax.Precision.HIGHEST,
        preferred_element_type=jnp.float32,
    )


def solve_kernel(row_ref, packed_ref, out_ref, coords_ref):
    half = packed_ref.shape[1]
    columns = half // 2
    scale = 1.0 / jnp.broadcast_to(packed_ref[0:1, 0:1], (8, half))
    row_blocks = lambda base: [packed_ref[base + 8 * i : base + 8 * i + 8] * scale for i in range(half // 8)]
    low_left = jnp.concatenate(row_blocks(half), axis=0)
    right = jnp.concatenate(row_blocks(3 * half), axis=0)
    first_inv = inverse(row_blocks(0))
    cross = precise_dot(first_inv, low_left, (1, 1))
    first = precise_dot(first_inv, right)
    schur = jnp.concatenate(row_blocks(2 * half), axis=0) - precise_dot(low_left, cross)
    rest = right[:, columns:] - precise_dot(low_left, first[:, :columns])
    second_inv = inverse([schur[8 * i : 8 * i + 8] for i in range(half // 8)])
    second = precise_dot(second_inv, rest)
    coords_ref[half:] = second
    coords_ref[:half] = first[:, :columns] - precise_dot(cross, second)
    out_ref[...] = coords_ref[pl.ds(row_ref[0], 1)]


def solved_row(packed, row):
    half = packed.shape[1]
    return pl.pallas_call(
        solve_kernel,
        out_shape=jax.ShapeDtypeStruct((1, half // 2), jnp.float32),
        in_specs=[pl.BlockSpec(memory_space=pltpu.SMEM), pl.BlockSpec(memory_space=pltpu.VMEM)],
        out_specs=pl.BlockSpec(memory_space=pltpu.VMEM),
        scratch_shapes=[pltpu.VMEM((2 * half, half // 2), jnp.float32)],
        name="solve",
    )(row, packed)

NT = (((1,), (1,)), ((), ()))

def rows_to_front(scratch_ref, value, count):
    n, eight, lanes = value.shape
    scratch_ref[: n * eight] = value.reshape(n * eight, lanes)
    return jnp.concatenate(
        [scratch_ref[pl.ds(q, count, stride=eight)].astype(jnp.bfloat16) for q in range(eight)], axis=1
    )

def gram_kernel(modes_ref, history_ref, mass_ref, gram_ref, projected_ref, weighted_ref, ws, ms, ss):
    step = pl.program_id(0)

    @pl.when(step == 0)
    def _():
        gram_ref[...] = jnp.zeros_like(gram_ref)
        projected_ref[...] = jnp.zeros_like(projected_ref)
        ss[...] = jnp.zeros_like(ss)

    modes = modes_ref[:, 0].astype(jnp.float32)
    count = modes.shape[0]
    weighted = rows_to_front(ws, modes * mass_ref[...][None], count)
    weighted_ref[0] = weighted
    plain = rows_to_front(ms, modes, count)
    gram_ref[...] += lax.dot_general(weighted, plain, NT, preferred_element_type=jnp.float32)
    history = rows_to_front(ss, history_ref[:, 0].astype(jnp.float32), projected_ref.shape[1])
    projected_ref[...] += lax.dot_general(weighted, history, NT, preferred_element_type=jnp.float32)


def gram(modes, history, mass):
    count, comps, rows, lanes = modes.shape
    earlier = history.shape[0]
    snaps = 64
    tiles = rows // 8
    return pl.pallas_call(
        gram_kernel,
        grid=(comps * tiles,),
        in_specs=[
            pl.BlockSpec((count, 1, 8, lanes), lambda i: (0, i // tiles, i % tiles, 0)),
            pl.BlockSpec((earlier, 1, 8, lanes), lambda i: (0, i // tiles, i % tiles, 0)),
            pl.BlockSpec((8, lanes), lambda i: (i % tiles, 0)),
        ],
        out_specs=[
            pl.BlockSpec((count, count), lambda i: (0, 0)),
            pl.BlockSpec((count, snaps), lambda i: (0, 0)),
            pl.BlockSpec((1, count, 8 * lanes), lambda i: (i, 0, 0)),
        ],
        out_shape=[
            jax.ShapeDtypeStruct((count, count), jnp.float32),
            jax.ShapeDtypeStruct((count, snaps), jnp.float32),
            jax.ShapeDtypeStruct((comps * tiles, count, 8 * lanes), jnp.bfloat16),
        ],
        scratch_shapes=[
            pltpu.VMEM((count * 8, lanes), jnp.float32),
            pltpu.VMEM((count * 8, lanes), jnp.float32),
            pltpu.VMEM((snaps * 8, lanes), jnp.float32),
        ],
        compiler_params=pltpu.CompilerParams(vmem_limit_bytes=24 << 20),
        cost_estimate=pl.CostEstimate(flops=2 * count * (count + snaps) * comps * rows * lanes, bytes_accessed=18 << 20, transcendentals=0),
        name="gram",
    )(modes, history, mass)


def pack_kernel(weighted_ref, u1, u2, u3, u4, gram_ref, projected_ref, packed_ref, acc):
    step = pl.program_id(0)

    @pl.when(step == 0)
    def _():
        acc[...] = jnp.zeros_like(acc)

    news = [u[0] for u in (u1, u2, u3, u4)]
    blank = jnp.zeros((8 - len(news), news[0].shape[1]), jnp.float32)
    rows = jnp.concatenate(
        [
            jnp.concatenate([new[q : q + 1] for new in news] + [blank], axis=0).astype(jnp.bfloat16)
            for q in range(8)
        ],
        axis=1,
    )
    acc[...] += lax.dot_general(weighted_ref[0], rows, NT, preferred_element_type=jnp.float32)

    @pl.when(step == pl.num_programs(0) - 1)
    def _():
        half = packed_ref.shape[1]
        first, last = gram_ref[:half, :half], gram_ref[half:, half:]
        packed_ref[:half] = 0.5 * (first + first.T)
        packed_ref[half : 2 * half] = 0.5 * (gram_ref[half:, :half] + gram_ref[:half, half:].T)
        packed_ref[2 * half : 3 * half] = 0.5 * (last + last.T)
        earlier = projected_ref.shape[1] - len(news)
        own = jnp.concatenate([projected_ref[:, :earlier], acc[:, : len(news)]], axis=1)
        packed_ref[3 * half :] = jnp.concatenate([own[:half], own[half:]], axis=1)


def packed_sums(weighted, states, gram_own, projected):
    chunks, count, width = weighted.shape
    rows, lanes = states[0].shape[1:]
    tiles = rows // 8
    half = count // 2
    state_spec = pl.BlockSpec((1, 8, lanes), lambda i: (i // tiles, i % tiles, 0))
    whole = lambda a: pl.BlockSpec(a.shape, lambda i: (0,) * a.ndim)
    return pl.pallas_call(
        pack_kernel,
        grid=(chunks,),
        in_specs=[pl.BlockSpec((1, count, width), lambda i: (i, 0, 0))]
        + [state_spec] * len(states)
        + [whole(gram_own), whole(projected)],
        out_specs=pl.BlockSpec((4 * half, half), lambda i: (0, 0)),
        out_shape=jax.ShapeDtypeStruct((4 * half, half), jnp.float32),
        scratch_shapes=[pltpu.VMEM((count, 8), jnp.float32)],
        compiler_params=pltpu.CompilerParams(vmem_limit_bytes=24 << 20),
        cost_estimate=pl.CostEstimate(flops=2 * count * 64 * 15360, bytes_accessed=9 << 20, transcendentals=0),
        name="pack",
    )(weighted, *states, gram_own, projected)

time_step = 0.3
mass_damping = 0.1
stiff_damping = 0.05
shear_stiff = 0.5
axial_components = (2, 1, 0)
FIBRES = 8


def edge_kernel(disp_ref, velo_ref, plastic_ref, harden_ref, ids_ref, up_ref, down_ref, left_ref, right_ref):
    lane = lax.broadcasted_iota(jnp.int32, left_ref.shape, 1)
    last = left_ref.shape[1] - 1
    left = jnp.zeros(left_ref.shape, jnp.float32)
    right = jnp.zeros(left_ref.shape, jnp.float32)
    for c in range(6):
        field = disp_ref[c] if c < 3 else velo_ref[c - 3]
        up_ref[c] = field
        down_ref[c] = field
        left = jnp.where(lane == c, pltpu.roll(field, c, 1) if c else field, left)
        right = jnp.where(lane == c, pltpu.roll(field, (c - last) % (last + 1), 1), right)
    for f in range(FIBRES):
        own = (plastic_ref, harden_ref, ids_ref)
        for k, ref in enumerate(own):
            down_ref[6 + FIBRES * k + f] = ref[f].astype(jnp.float32)
            target = 8 + FIBRES * k + f
            left = jnp.where(lane == target, pltpu.roll(ref[2 * FIBRES + f].astype(jnp.float32), target, 1), left)
    left_ref[...] = left
    right_ref[...] = right


def chosen(ids, values):
    low, mid, high = ((ids & bit) != 0 for bit in (1, 2, 4))
    pairs = [jnp.where(low, values[2 * i + 1], values[2 * i]) for i in range(4)]
    return jnp.where(high, jnp.where(mid, pairs[3], pairs[2]), jnp.where(mid, pairs[1], pairs[0]))


def material(ids, table_ref):
    modulus = chosen(ids, [table_ref[i, 0] for i in range(8)])
    yields = chosen(ids, [0.4 * table_ref[i, 1] for i in range(8)])
    slopes = chosen(ids, [0.1 * table_ref[i, 2] for i in range(8)])
    return modulus, yields, slopes, 1.0 / (modulus + slopes)


def fibre_step(stretch, plastic, harden, props):
    modulus, yields, slopes, inverse = props
    trial = modulus * (stretch - plastic)
    growth = jnp.maximum(jnp.abs(trial) - (yields + slopes * harden), 0.0) * inverse
    signed = jnp.where(trial >= 0.0, growth, -growth)
    return trial - modulus * signed, plastic + signed, harden + growth


def step_kernel(first, last, step, *refs):
    refs = list(refs)
    take = lambda n: [refs.pop(0) for _ in range(n)]
    top_ref, accel_ref, table_ref = take(3)
    if first:
        disp_in, velo_in = take(2)
        now = [disp_in.at[c] for c in range(3)] + [velo_in.at[c] for c in range(3)]
    else:
        (state_in,) = take(1)
        now = [state_in.at[c] for c in range(6)]
    below_ref, above_ref, left_ref, right_ref, mass_ref, plastic_in, harden_in = take(7)
    if first:
        (ids_ref,) = take(1)
    else:
        above_fib, side_fib, props_ref, tangent_ref = take(4)
    if last:
        disp_out, velo_out = take(2)
    else:
        (state_out,) = take(1)
    plastic_out, harden_out = take(2)
    if not last:
        left_out, right_out, above_out, side_out = take(4)
    if first:
        props_out, tangent_out = take(2)

    rows, lanes = left_ref.shape
    lane = lax.broadcasted_iota(jnp.int32, (rows, lanes), 1)
    row = lax.broadcasted_iota(jnp.int32, (rows, lanes), 0)
    u = [now[c][...] for c in range(3)]
    v = [now[c + 3][...] for c in range(3)]

    def props_of(index, ids):
        if first:
            props = material(ids(), table_ref)
            if not last:
                for k in range(4):
                    props_out[k, index] = props[k]
            return props
        return [props_ref[k, index] for k in range(4)]

    def axial_force(bar, stretch, rate):
        total = jnp.zeros((rows, lanes), jnp.float32)
        modulus_sum = jnp.zeros((rows, lanes), jnp.float32)
        for f in range(FIBRES):
            index = FIBRES * bar + f
            if bar < 3:
                plastic, harden = plastic_in[index], harden_in[index]
                ids = lambda: ids_ref[index]
            elif first:
                plastic, harden = above_ref[6 + f], above_ref[6 + FIBRES + f]
                ids = lambda: above_ref[6 + 2 * FIBRES + f].astype(jnp.int32)
            else:
                plastic, harden = above_fib[0, f], above_fib[1, f]
                ids = None
            props = props_of(index, ids)
            stress, plastic, harden = fibre_step(stretch, plastic, harden, props)
            if bar < 3:
                plastic_out[index] = plastic
                harden_out[index] = harden
            elif not last:
                above_out[0, f] = plastic
                above_out[1, f] = harden
            total = total + stress
            if first:
                modulus_sum = modulus_sum + props[0]
        if first:
            tangent = (stiff_damping / FIBRES) * modulus_sum
            if not last:
                tangent_out[bar] = tangent
        else:
            tangent = tangent_ref[bar]
        return (1.0 / FIBRES) * total + tangent * rate

    def shear_force(stretch, rate):
        return shear_stiff * (stretch + stiff_damping * rate)

    def bar_force(bar, stretch, rate):
        axial = axial_components[min(bar, 3) % 3]
        return [
            axial_force(bar, stretch[c], rate[c]) if c == axial else shear_force(stretch[c], rate[c])
            for c in range(3)
        ]

    own = bar_force(0, [u[c] - below_ref[c] for c in range(3)], [v[c] - below_ref[c + 3] for c in range(3)])
    later = bar_force(3, [above_ref[c] - u[c] for c in range(3)], [above_ref[c + 3] - v[c] for c in range(3)])
    has_later = jnp.where(top_ref[0] == 0, 1.0, 0.0)
    resisting = [own[c] - has_later * later[c] for c in range(3)]

    shift = lambda x: jnp.where(row == 0, 0.0, pltpu.roll(x, 1, 0))
    own = bar_force(1, [x - shift(x) for x in u], [x - shift(x) for x in v])
    for c in range(3):
        resisting[c] = resisting[c] + own[c] - jnp.where(row == rows - 1, 0.0, pltpu.roll(own[c], rows - 1, 0))

    left, right = left_ref[...], right_ref[...]

    def behind(x, c):
        return jnp.where(lane == 0, pltpu.roll(left, (lanes - c) % lanes, 1) if c else left, pltpu.roll(x, 1, 1))

    own = bar_force(
        2, [u[c] - behind(u[c], c) for c in range(3)], [v[c] - behind(v[c], c + 3) for c in range(3)]
    )
    column = lambda x, c: jnp.broadcast_to(x[:, c : c + 1], (rows, lanes))
    stretch = [column(right, c) - column(u[c], lanes - 1) for c in range(3)]
    rate = [column(right, c + 3) - column(v[c], lanes - 1) for c in range(3)]
    if first:
        plastic, harden = pltpu.roll(right, lanes - 8, 1), pltpu.roll(right, lanes - 16, 1)
        props = props_of(4 * FIBRES, lambda: pltpu.roll(right, lanes - 24, 1).astype(jnp.int32) & 7)
        tangent = jnp.sum(jnp.where(lane < FIBRES, props[0], 0.0), axis=1, keepdims=True)
        tangent = jnp.broadcast_to((stiff_damping / FIBRES) * tangent, (rows, lanes))
        if not last:
            tangent_out[4] = tangent
    else:
        plastic, harden = side_fib[0], side_fib[1]
        props = props_of(4 * FIBRES, None)
        tangent = tangent_ref[4]
    stress, plastic, harden = fibre_step(stretch[0], plastic, harden, props)
    if not last:
        side_out[0] = plastic
        side_out[1] = harden
    axial = jnp.sum(jnp.where(lane < FIBRES, stress, 0.0), axis=1, keepdims=True)
    side = [
        jnp.broadcast_to((1.0 / FIBRES) * axial, (rows, lanes)) + tangent * rate[0],
        shear_force(stretch[1], rate[1]),
        shear_force(stretch[2], rate[2]),
    ]
    inverse_mass = 1.0 / mass_ref[...]
    new_left = jnp.zeros((rows, lanes), jnp.float32)
    new_right = jnp.zeros((rows, lanes), jnp.float32)
    for c in range(3):
        ahead = jnp.where(lane == lanes - 1, side[c], pltpu.roll(own[c], lanes - 1, 1))
        force = resisting[c] + own[c] - ahead
        acceleration = -accel_ref[step, c] - force * inverse_mass
        velo = ((1.0 - 0.5 * mass_damping * time_step) * v[c] + time_step * acceleration) * (
            1.0 / (1.0 + 0.5 * mass_damping * time_step)
        )
        disp = u[c] + time_step * velo
        if last:
            disp_out[c] = disp
            velo_out[c] = velo
        else:
            state_out[c] = disp
            state_out[c + 3] = velo
            for k, field in ((c, disp), (c + 3, velo)):
                new_left = jnp.where(lane == k, pltpu.roll(field, k, 1) if k else field, new_left)
                new_right = jnp.where(lane == k, pltpu.roll(field, (k + 1) % lanes, 1), new_right)
    if not last:
        left_out[...] = new_left
        right_out[...] = new_right


def call(kernel, outs, args, smem, name, aliases=()):
    shape = lambda s: jax.ShapeDtypeStruct(s, jnp.float32)
    specs = [pl.BlockSpec(memory_space=pltpu.SMEM)] * smem + [pl.BlockSpec(memory_space=pltpu.VMEM)] * (len(args) - smem)
    return pl.pallas_call(
        kernel,
        in_specs=specs,
        out_specs=[pl.BlockSpec(memory_space=pltpu.VMEM)] * len(outs),
        out_shape=[shape(s) for s in outs],
        compiler_params=pltpu.CompilerParams(vmem_limit_bytes=28 << 20),
        cost_estimate=pl.CostEstimate(flops=10_000_000, bytes_accessed=5 << 20, transcendentals=0),
        name=name,
    )(*args)


def edges(disp, velo, plastic, harden, ids):
    _, rows, lanes = disp.shape
    return call(
        edge_kernel,
        [(6, rows, lanes), (6 + 3 * FIBRES, rows, lanes), (rows, lanes), (rows, lanes)],
        (disp, velo, plastic, harden, ids),
        0,
        "edges",
    )


def run_steps(disp, velo, mass, plastic, harden, ids, table, accel, top, send_up, send_down, send_left, send_right):
    steps = accel.shape[0]
    _, rows, lanes = disp.shape
    tile = (rows, lanes)
    up, down, left, right = edges(disp, velo, plastic, harden, ids)
    states = []
    for n in range(steps):
        first, last = n == 0, n == steps - 1
        below, above = send_up(up), send_down(down)
        from_left, from_right = send_right(right), send_left(left)
        now = (disp, velo) if first else (state,)
        extra = (ids,) if first else (above_fib, side_fib, props, tangent)
        outs = ([(3,) + tile, (3,) + tile] if last else [(6,) + tile]) + [plastic.shape, harden.shape]
        if not last:
            outs += [tile, tile, (2, FIBRES) + tile, (2,) + tile]
        if first:
            outs += [(4, 4 * FIBRES + 1) + tile, (5,) + tile]
        results = list(
            call(
                functools.partial(step_kernel, first, last, n),
                outs,
                (top, accel, table) + now + (below, above, from_left, from_right, mass, plastic, harden) + extra,
                3,
                "step",
            )
        )
        if last:
            disp, velo, plastic, harden = results
            states.append(disp)
        else:
            state, plastic, harden, left, right, above_fib, side_fib = results[:7]
            up = down = state
            states.append(state)
        if first:
            props, tangent = results[7:]
    return disp, velo, plastic, harden, states


def passed_along(block, axis, distance):
    devices = range(lax.axis_size(axis))
    route = [(i - distance, i) for i in devices if i - distance in devices]
    return lax.ppermute(block, axis, route)


def from_behind(block, axis, distance):
    devices = range(lax.axis_size(axis))
    route = [((i - distance) % len(devices), i) for i in devices]
    return lax.ppermute(block, axis, route)


def summed_over_devices(packed):
    first, second = lax.axis_size(FIRST), lax.axis_size(SECOND)
    pieces = packed.reshape(first, packed.shape[0] // first, packed.shape[1])
    own = jnp.sum(lax.all_to_all(pieces, FIRST, 0, 0, tiled=True), axis=0)
    spread = jnp.broadcast_to(own[None], (second,) + own.shape)
    total = jnp.sum(lax.all_to_all(spread, SECOND, 0, 0, tiled=True), axis=0)
    spread = jnp.broadcast_to(total[None], (first,) + total.shape)
    return lax.all_to_all(spread, FIRST, 0, 0, tiled=True).reshape(packed.shape)


def body(
    displacement,
    velocity,
    lumped_mass,
    plastic_strain,
    hardening_strain,
    material_ids,
    material_table,
    ground_accel,
    snapshot_history,
    mode_shapes,
):
    rows, lanes = lumped_mass.shape[1:]
    mass = lumped_mass.reshape(rows, lanes)
    fibres = lambda x: x.reshape(-1, rows, lanes)
    modes = mode_shapes.reshape(-1, 3, rows, lanes)
    history = snapshot_history.reshape(-1, 3, rows, lanes)
    top = (lax.axis_index(HEIGHT) == lax.axis_size(HEIGHT) - 1).astype(jnp.int32).reshape(1)
    gram_own, projected, weighted = gram(modes, history, mass)
    disp, velo, plastic, harden, states = run_steps(
        fibres(displacement),
        fibres(velocity),
        mass,
        fibres(plastic_strain),
        fibres(hardening_strain),
        fibres(material_ids),
        material_table,
        ground_accel,
        top,
        lambda x: passed_along(x, HEIGHT, 1),
        lambda x: passed_along(x, HEIGHT, -1),
        lambda x: from_behind(x, PLAN, -1),
        lambda x: from_behind(x, PLAN, 1),
    )
    packed = summed_over_devices(packed_sums(weighted, states, gram_own, projected))
    index = lax.axis_index(HEIGHT + PLAN).astype(jnp.int32).reshape(1)
    modal_coords = solved_row(packed, index)
    return (
        disp.reshape(displacement.shape),
        velo.reshape(velocity.shape),
        plastic.reshape(plastic_strain.shape),
        harden.reshape(hardening_strain.shape),
        modal_coords,
    )


def solution(mesh):
    return jax.shard_map(
        body,
        mesh=jax.sharding.Mesh(mesh.devices.reshape(4, 4, 2, 2, 4), HEIGHT + PLAN),
        in_specs=(
            P(None, HEIGHT, None, PLAN),
            P(None, HEIGHT, None, PLAN),
            P(HEIGHT, None, PLAN),
            P(None, None, HEIGHT, None, PLAN),
            P(None, None, HEIGHT, None, PLAN),
            P(None, None, HEIGHT, None, PLAN),
            P(),
            P(),
            P(None, None, HEIGHT, None, PLAN),
            P(None, None, HEIGHT, None, PLAN),
        ),
        out_specs=(
            P(None, HEIGHT, None, PLAN),
            P(None, HEIGHT, None, PLAN),
            P(None, None, HEIGHT, None, PLAN),
            P(None, None, HEIGHT, None, PLAN),
            P(HEIGHT + PLAN, None),
        ),
        check_vma=False,
    )
```
